32 devices in a mesh: grp: 4 (over x, core), tile: 8 (over z, y).
Axes of the slice: x: 2, y: 2, z: 4, core: 2. Of those that a mesh axis runs over, the one named last changes fastest.
Arguments:
- factors: bfloat16 [4096, 128, 128], P('tile', 'grp'), may hold values from -0.09375 to 0.09375
- amplitudes: bfloat16 [512, 128, 128], P('tile', 'grp'), may hold values from -6 to 6
- tile_mask: int32 [8, 2, 2], replicated, may hold values 0 or 1
Outputs:
- residual: bfloat16 [128, 64, 512], P('tile', None, 'grp')
The draws below stay inside these ranges and needn't reach their ends.
All inputs are finite; a program needn't handle non-finite values.
Results may differ from the reference program's by a relative error of at most 0.011.
Values may be sent and summed in bfloat16 or wider, within the bound.
No kernel may reach another device: no remote copies, remote signals or barrier semaphores. Data moves between devices by JAX's collectives and lax.ppermute only.
A program may use at most 128 MiB of HBM per device.

```python
import jax
import jax.numpy as jnp
from jax import lax

NAUX = 4096
NV = 128
VB = 64
NB = 64
IJB = 64
PAIRS = 512
NVB = 2
NBLK = 8


def with_ends(drawn, key, least, high):
    longest = drawn.shape.index(max(drawn.shape))
    spots = []
    for shift in (0, 1):
        where = [jax.random.randint(jax.random.fold_in(key, axis), (), 0, length) for axis, length in enumerate(drawn.shape)]
        where[longest] = (where[longest] + shift) % drawn.shape[longest]
        spots.append(tuple(where))
    return drawn.at[spots[0]].set(least).at[spots[1]].set(high)


def block_levels(key, extent, cuts, low, high):
    loudness = 1.0
    for dim, parts in cuts:
        steps = jax.random.uniform(jax.random.fold_in(jax.random.fold_in(key, 6), dim), (parts,), jnp.float32, low / len(cuts), high / len(cuts))
        loudness = loudness * jnp.repeat(jnp.exp(steps), extent[dim] // parts).reshape((-1,) + (1,) * (len(extent) - 1 - dim))
    return loudness


def scatter_about(key, shape, width, most, cuts=(), kind=jnp.bfloat16):
    factor_of = block_levels(key, shape, cuts, -0.22, 0.18) if cuts else 1.0
    array = jax.random.normal(key, shape, jnp.float32) * width * factor_of
    return jnp.minimum(jnp.maximum(array, -most), most).astype(kind)


def setup_inputs(seed: int = 0) -> dict:
    splits = jax.random.split(jax.random.key(seed), 4)
    return {
        "factors": scatter_about(splits[0], (NAUX, NV, NV), NAUX ** -0.5, 0.09375, ((0, 8), (1, 4))),
        "amplitudes": scatter_about(splits[1], (PAIRS, NV, NV), 1.0, 6.0, ((0, 8), (1, 4))),
        "tile_mask": with_ends((jax.random.randint(splits[2], (NBLK, NVB, NVB), 0, 2) < 1).astype(jnp.int32), jax.random.fold_in(splits[2], 1), 0, 1),
    }


def reference(factors, amplitudes, tile_mask):
    block_width = 8
    pair_blocks = jnp.arange(PAIRS, dtype=jnp.int32) // IJB
    virt_blocks = jnp.arange(NV, dtype=jnp.int32) // VB
    by_pair = tile_mask[pair_blocks]
    amp_mask = by_pair[:, virt_blocks][:, :, virt_blocks].transpose(0, 2, 1)
    res_mask = by_pair[:, virt_blocks][:, :, virt_blocks[:NB]].transpose(1, 2, 0)
    screened = amplitudes * amp_mask.astype(jnp.bfloat16)
    window = factors[:, :, :NB].reshape(NAUX, NV * NB)

    def add_block(index, total):
        start = (index * block_width).astype(jnp.int32)
        left_part = lax.dynamic_slice_in_dim(factors, start, block_width, 1)
        left_part = left_part.reshape(NAUX, block_width * NV)
        gram = lax.dot_general(left_part, window, (((0,), (0,)), ((), ())), preferred_element_type=jnp.float32)
        integrals = gram.astype(jnp.bfloat16).reshape(block_width, NV, NV, NB).transpose(0, 2, 1, 3)
        integrals = integrals.reshape(block_width * NV, NV * NB)
        amps = lax.dynamic_slice_in_dim(screened, start, block_width, 2).transpose(0, 2, 1)
        amps = amps.reshape(PAIRS, block_width * NV)
        return total + jnp.dot(amps, integrals, preferred_element_type=jnp.float32)

    ladder = lax.fori_loop(0, NV // block_width, add_block, jnp.zeros((PAIRS, NV * NB), jnp.float32))
    ladder = ladder.reshape(PAIRS, NV, NB).transpose(1, 2, 0)
    return (ladder * res_mask.astype(jnp.float32)).astype(jnp.bfloat16)
```

```python
import jax
import jax.numpy as jnp
from jax import lax
from jax.experimental import pallas as pl
from jax.experimental.pallas import tpu as pltpu
from jax.sharding import PartitionSpec as P

VB = 64
NB = 64
IJB = 64
CHUNKS = 4
CGROUP = 8


def integrals_kernel(*refs):
    left_ref, *piece_refs, out_ref = refs
    bs, d_part, aux = piece_refs[0].shape
    d_all = d_part * len(piece_refs)
    step = max(1, 256 // d_all)
    c_here = out_ref.shape[1] // d_all
    a_all = left_ref.shape[0] // c_here

    def body(i, carry):
        parts = []
        for j in range(step):
            for ref in piece_refs:
                parts.append(ref[i * step + j])
        right = jnp.concatenate(parts, axis=0)
        gram = lax.dot_general(
            left_ref[...], right, (((1,), (1,)), ((), ())), preferred_element_type=jnp.float32
        ).astype(jnp.bfloat16)
        for j in range(step):
            start = pl.multiple_of((i * step + j) * a_all, a_all)
            for c in range(c_here):
                out_ref[pl.ds(start, a_all), c * d_all : (c + 1) * d_all] = gram[
                    c * a_all : (c + 1) * a_all, j * d_all : (j + 1) * d_all
                ]
        return carry

    lax.fori_loop(0, bs // step, body, 0)


def partial_integrals(left, pieces, c_all):
    rows, aux = left.shape
    a_all = rows // c_all
    bs, d_part, _ = pieces[0].shape
    d_all = d_part * len(pieces)
    group = min(CGROUP, c_all)
    piece_spec = pl.BlockSpec((bs, d_part, aux), lambda i: (0, 0, 0))
    return pl.pallas_call(
        integrals_kernel,
        grid=(c_all // group,),
        in_specs=[pl.BlockSpec((group * a_all, aux), lambda i: (i, 0))] + [piece_spec] * len(pieces),
        out_specs=pl.BlockSpec((bs * a_all, group * d_all), lambda i: (0, i)),
        out_shape=jax.ShapeDtypeStruct((bs * a_all, c_all * d_all), jnp.bfloat16),
        cost_estimate=pl.CostEstimate(
            flops=2 * rows * aux * bs * d_all,
            bytes_accessed=2 * (rows * aux + bs * d_all * (aux + rows)),
            transcendentals=0,
        ),
        compiler_params=pltpu.CompilerParams(vmem_limit_bytes=48 * 1024 * 1024),
        name="partial_integrals",
    )(left, *pieces)


def pick(x, index, axis):
    return lax.dynamic_index_in_dim(x, index, axis, keepdims=False)


def on_device(factors, amplitudes, tile_mask):
    aux, quarter, virtuals = factors.shape
    tiles, groups = lax.axis_size("tile"), lax.axis_size("grp")
    tile, grp = lax.axis_index("tile"), lax.axis_index("grp")
    low, inner = 2, 2
    high, outer = groups // low, tiles // inner
    core, chip_x = grp % low, grp // low
    near, far = tile % inner, tile // inner
    a_local = virtuals // tiles
    rows = amplitudes.shape[0]
    pairs = rows * tiles
    pair_quarter = pairs // groups
    f32, bf16 = jnp.float32, jnp.bfloat16

    def shift(x, by_high=0, by_low=0, by_far=0, by_near=0):
        pairs_of = []
        for g in range(groups):
            for t in range(tiles):
                h, l = (g // low + by_high) % high, (g % low + by_low) % low
                o, i = (t // inner + by_far) % outer, (t % inner + by_near) % inner
                pairs_of.append((g * tiles + t, (h * low + l) * tiles + o * inner + i))
        return lax.ppermute(x, ("grp", "tile"), pairs_of)

    pair_rows = tile * rows + jnp.arange(rows, dtype=jnp.int32)
    c_blocks = jnp.arange(virtuals, dtype=jnp.int32) // VB
    d_blocks = (grp * quarter + jnp.arange(quarter, dtype=jnp.int32)) // VB
    amp_mask = tile_mask[pair_rows // IJB][:, c_blocks][:, :, d_blocks].transpose(0, 2, 1)
    screened = amplitudes * amp_mask.astype(bf16)
    by_c = screened.reshape(rows, quarter, high, low, quarter).transpose(2, 3, 0, 4, 1)
    by_c = by_c.reshape(high, low, rows, quarter * quarter)
    mine = pick(by_c, core, 1)
    theirs = shift(pick(by_c, 1 - core, 1), by_low=1)
    both = jnp.stack([mine, theirs])
    amp_pieces = []
    for k in range(high):
        part = pick(both, (chip_x + k) % high, 1)
        amp_pieces.append(shift(part, by_high=k) if k else part)
    amps = jnp.concatenate(amp_pieces).reshape(groups, rows, quarter, quarter)
    amps = amps.transpose(1, 2, 0, 3).reshape(rows, quarter * virtuals)
    amps = lax.all_gather(amps, "tile", axis=0, tiled=True)

    left = factors.reshape(aux, quarter * virtuals).T
    window = left.reshape(quarter, virtuals, aux)[:, :NB].transpose(1, 0, 2)

    size = NB // CHUNKS
    chunks = []
    for n in range(CHUNKS):
        own = window[n * size : (n + 1) * size]
        held = [own] + [shift(own, by_high=k) for k in range(1, high)]
        swapped = shift(jnp.stack(held), by_low=1)
        pieces = []
        for k in range(high):
            pieces += [held[k], swapped[k]]
        integrals = partial_integrals(left, pieces, quarter)
        ladder = lax.dot_general(
            integrals, amps, (((1,), (1,)), ((), ())), preferred_element_type=f32
        ).reshape(size * virtuals, high, low, pair_quarter)
        mine = pick(ladder, core, 2)
        theirs = shift(pick(ladder, 1 - core, 2).astype(bf16), by_low=1)
        total = (mine + theirs.astype(f32)).astype(bf16)
        total = total.reshape(size, outer, inner, a_local, high, pair_quarter)
        acc = None
        for kx in range(high):
            for ky in range(inner):
                part = pick(pick(total, (chip_x + kx) % high, 4), (near + ky) % inner, 2)
                part = shift(part, by_high=kx, by_near=ky) if kx or ky else part
                acc = part.astype(f32) if acc is None else acc + part.astype(f32)
        total = acc.astype(bf16)
        acc = None
        for kz in range(outer):
            part = pick(total, (far + kz) % outer, 1)
            part = shift(part, by_far=kz) if kz else part
            acc = part.astype(f32) if acc is None else acc + part.astype(f32)
        chunks.append(acc.transpose(1, 0, 2))
    summed = jnp.concatenate(chunks, axis=1)

    out_rows = grp * pair_quarter + jnp.arange(pair_quarter, dtype=jnp.int32)
    a_blocks = (tile * a_local + jnp.arange(a_local, dtype=jnp.int32)) // VB
    b_blocks = jnp.arange(NB, dtype=jnp.int32) // VB
    res_mask = tile_mask[out_rows // IJB][:, a_blocks][:, :, b_blocks].transpose(1, 2, 0)
    return (summed * res_mask.astype(f32)).astype(bf16)


def solution(mesh):
    placed = (P("tile", "grp", None), P("tile", "grp", None), P())
    return jax.shard_map(
        on_device, mesh=mesh, in_specs=placed, out_specs=P("tile", None, "grp"), check_vma=False
    )
```

```python
import jax
import jax.numpy as jnp
from jax import lax
from jax.experimental import pallas as pl
from jax.experimental.pallas import tpu as pltpu
from jax.sharding import PartitionSpec as P


VB = 64
NB = 64
IJB = 64
SPLIT = (16, 24, 24)
CGROUP = 4
ROW_BLOCK = 512
VMEM_BYTES = 60 * 1024 * 1024


def integrals_kernel(*refs):
    left_ref, *piece_refs, out_ref = refs
    bs, d_part, _ = piece_refs[0].shape
    d_all = d_part * len(piece_refs)
    c_here = out_ref.shape[1] // d_all
    a_all = left_ref.shape[0] // c_here
    step = 8
    for i in range(0, bs, step):
        right = jnp.concatenate([ref[i + j] for j in range(step) for ref in piece_refs], axis=0)
        gram = lax.dot_general(
            left_ref[...], right, (((1,), (1,)), ((), ())), preferred_element_type=jnp.float32
        ).astype(jnp.bfloat16)
        for j in range(step):
            for c in range(c_here):
                out_ref[(i + j) * a_all : (i + j + 1) * a_all, c * d_all : (c + 1) * d_all] = gram[
                    c * a_all : (c + 1) * a_all, j * d_all : (j + 1) * d_all
                ]


def partial_integrals(left, pieces, c_all):
    rows, aux = left.shape
    a_all = rows // c_all
    bs, d_part, _ = pieces[0].shape
    d_all = d_part * len(pieces)
    piece_spec = pl.BlockSpec((bs, d_part, aux), lambda i: (0, 0, 0))
    return pl.pallas_call(
        integrals_kernel,
        grid=(c_all // CGROUP,),
        in_specs=[pl.BlockSpec((CGROUP * a_all, aux), lambda i: (i, 0))] + [piece_spec] * len(pieces),
        out_specs=pl.BlockSpec((bs * a_all, CGROUP * d_all), lambda i: (0, i)),
        out_shape=jax.ShapeDtypeStruct((bs * a_all, c_all * d_all), jnp.bfloat16),
        cost_estimate=pl.CostEstimate(
            flops=2 * rows * aux * bs * d_all,
            bytes_accessed=2 * (rows * aux + bs * d_all * (aux + rows)),
            transcendentals=0,
        ),
        compiler_params=pltpu.CompilerParams(vmem_limit_bytes=VMEM_BYTES),
        name="partial_integrals",
    )(left, *pieces)


def ladder_kernel(place_ref, integrals_ref, amps_ref, keep_ref, send_ref):
    high, quarter = keep_ref.shape[0], keep_ref.shape[-1]
    low = 2
    core, chip_x, near = place_ref[0], place_ref[1], place_ref[2]
    half = lax.dot_general(
        integrals_ref[...], amps_ref[...], (((1,), (1,)), ((), ())), preferred_element_type=jnp.float32
    ).astype(jnp.bfloat16)
    for h in range(high):
        slot = lax.rem(h - chip_x + high, high)
        blocks = [
            half[:, (h * low + c) * quarter : (h * low + c + 1) * quarter] for c in range(low)
        ]
        keep = jnp.where(core == 0, blocks[0], blocks[1])
        send = jnp.where(core == 0, blocks[1], blocks[0])
        if len(keep_ref.shape) == 3:
            keep_ref[slot], send_ref[slot] = keep, send
            continue
        _, inner, outer, bs, a_local, _ = keep_ref.shape
        a_all = outer * inner * a_local
        for i in range(inner):
            at = lax.rem(i - near + inner, inner)
            for b in range(bs):
                for o in range(outer):
                    row = b * a_all + (o * inner + i) * a_local
                    keep_ref[slot, at, o, b] = keep[row : row + a_local]
                    send_ref[slot, at, o, b] = send[row : row + a_local]


def ladder(place, integrals, amps, high, low, split):
    rows, inner = integrals.shape
    pairs = amps.shape[0]
    quarter = pairs // (high * low)
    block = ROW_BLOCK * 512 // max(512, pairs)
    if split[-1] % 16:
        shape, piece = (high, rows, quarter), (high, block, quarter)
        spec = pl.BlockSpec(piece, lambda i, place: (0, i, 0))
    else:
        near, far, a_local = split
        a_all = near * far * a_local
        shape = (high, near, far, rows // a_all, a_local, quarter)
        piece = (high, near, far, block // a_all, a_local, quarter)
        spec = pl.BlockSpec(piece, lambda i, place: (0, 0, 0, i, 0, 0))
    shape = jax.ShapeDtypeStruct(shape, jnp.bfloat16)
    return pl.pallas_call(
        ladder_kernel,
        grid_spec=pltpu.PrefetchScalarGridSpec(
            num_scalar_prefetch=1,
            grid=(rows // block,),
            in_specs=[
                pl.BlockSpec((block, inner), lambda i, place: (i, 0)),
                pl.BlockSpec((pairs, inner), lambda i, place: (0, 0), pipeline_mode=pl.Buffered(1)),
            ],
            out_specs=[spec, spec],
        ),
        out_shape=[shape, shape],
        cost_estimate=pl.CostEstimate(
            flops=2 * rows * inner * pairs,
            bytes_accessed=2 * (rows * inner + pairs * inner + rows * pairs),
            transcendentals=0,
        ),
        compiler_params=pltpu.CompilerParams(vmem_limit_bytes=VMEM_BYTES),
        name="ladder",
    )(place, integrals, amps)


def pick(x, index, axis):
    return lax.dynamic_index_in_dim(x, index, axis, keepdims=False)


def on_device(factors, amplitudes, tile_mask):
    aux, quarter, virtuals = factors.shape
    tiles, groups = lax.axis_size("tile"), lax.axis_size("grp")
    tile, grp = lax.axis_index("tile"), lax.axis_index("grp")
    low, inner = 2, 2
    high, outer = groups // low, tiles // inner
    core, chip_x = grp % low, grp // low
    near, far = tile % inner, tile // inner
    a_local = virtuals // tiles
    rows = amplitudes.shape[0]
    pairs = rows * tiles
    pair_quarter = pairs // groups
    f32, bf16 = jnp.float32, jnp.bfloat16
    if rows % IJB or VB % quarter or pair_quarter % IJB or VB % a_local or VB != NB:
        raise ValueError("block sizes")

    def shift(x, by_high=0, by_low=0, by_far=0, by_near=0):
        pairs_of = []
        for g in range(groups):
            for t in range(tiles):
                h, l = (g // low + by_high) % high, (g % low + by_low) % low
                o, i = (t // inner + by_far) % outer, (t % inner + by_near) % inner
                pairs_of.append((g * tiles + t, (h * low + l) * tiles + o * inner + i))
        return lax.ppermute(x, ("grp", "tile"), pairs_of)

    kept = lax.dynamic_slice_in_dim(tile_mask, tile * (rows // IJB), rows // IJB, 0)
    kept = pick(kept, grp * quarter // VB, 2).astype(bf16)[:, None, None, :, None]
    screened = amplitudes.reshape(rows // IJB, IJB, quarter, virtuals // VB, VB) * kept
    by_c = screened.reshape(rows, quarter, virtuals).transpose(2, 1, 0)
    by_c = by_c.reshape(high, low, quarter, quarter * rows)
    mine = pick(by_c, core, 1)
    theirs = shift(pick(by_c, 1 - core, 1), by_low=1)
    both = jnp.stack([mine, theirs])
    amp_pieces = []
    for k in range(high):
        part = pick(both, (chip_x + k) % high, 1)
        amp_pieces.append(shift(part, by_high=k) if k else part)

    window = factors[:, :, :NB].transpose(2, 1, 0)
    window, *amp_pieces = lax.optimization_barrier((window, *amp_pieces))

    amps = jnp.concatenate(amp_pieces).reshape(groups, quarter, quarter, rows)
    amps = amps.transpose(3, 1, 0, 2).reshape(rows, quarter * virtuals)
    amps = lax.all_gather(amps, "tile", axis=0, tiled=True)
    left = factors.reshape(aux, quarter * virtuals).T

    starts = [sum(SPLIT[:n]) for n in range(len(SPLIT))]
    owns = [window[s : s + size] for s, size in zip(starts, SPLIT)]
    others = [[shift(own, by_high=k) for k in range(1, high)] for own in owns]
    integrals = []
    for n, own in enumerate(owns):
        held = [own] + others[n]
        if n:
            *held, integrals[-1] = lax.optimization_barrier((*held, integrals[-1]))
        pieces = []
        for piece in held:
            pieces += [piece, shift(piece, by_low=1)]
        integrals.append(partial_integrals(left, pieces, quarter))
    amps, *integrals = lax.optimization_barrier((amps, *integrals))

    place = jnp.stack([core, chip_x, near]).astype(jnp.int32)
    chunks = []
    for n, size in enumerate(SPLIT):
        keep, send = ladder(place, integrals[n], amps, high, low, (inner, outer, a_local))
        got = shift(send, by_low=1)
        parts = []
        for kx in range(high):
            for ky in range(inner):
                if keep.ndim == 6:
                    halves = [half[kx, ky] for half in (keep, got)]
                else:
                    view = (high, size, outer, inner, a_local, pair_quarter)
                    halves = [
                        pick(half.reshape(view)[kx], (near + ky) % inner, 2).swapaxes(0, 1)
                        for half in (keep, got)
                    ]
                parts.append((halves[0].astype(f32) + halves[1].astype(f32)).astype(bf16))
        if n + 1 < len(SPLIT):
            amps, *parts = lax.optimization_barrier((amps, *parts))
        total = None
        for kx in range(high):
            for ky in range(inner):
                part = parts[kx * inner + ky]
                if kx or ky:
                    part = shift(part, by_high=kx, by_near=ky)
                total = part.astype(f32) if total is None else total + part.astype(f32)
        total = total.astype(bf16)
        done = None
        for kz in range(outer):
            part = pick(total, (far + kz) % outer, 0)
            if kz:
                part = shift(part, by_far=kz)
            done = part.astype(f32) if done is None else done + part.astype(f32)
        chunks.append(done.transpose(1, 0, 2))
    summed = jnp.concatenate(chunks, axis=1)

    blocks = pair_quarter // IJB
    shown = lax.dynamic_slice_in_dim(tile_mask, grp * blocks, blocks, 0)[:, :, 0]
    shown = pick(shown, tile * a_local // VB, 1)
    shown = jnp.broadcast_to(shown[:, None], (blocks, IJB)).reshape(pair_quarter)
    return (summed * shown.astype(f32)).astype(bf16)


def solution(mesh):
    placed = (P("tile", "grp", None), P("tile", "grp", None), P())

    return jax.shard_map(
        on_device, mesh=mesh, in_specs=placed, out_specs=P("tile", None, "grp"), check_vma=False
    )
```

```python
import jax
import jax.numpy as jnp
from jax import lax
from jax.experimental import pallas as pl
from jax.experimental.pallas import tpu as pltpu
from jax.sharding import PartitionSpec as P


VB = 64
NB = 64
IJB = 64
SPLIT = (24, 24, 16)
CGROUP = 4
ROW_BLOCK = 512
VMEM_BYTES = 60 * 1024 * 1024


def integrals_kernel(*refs):
    left_ref, *piece_refs, out_ref = refs
    bs, d_part, _ = piece_refs[0].shape
    d_all = d_part * len(piece_refs)
    c_here = out_ref.shape[1] // d_all
    a_all = left_ref.shape[0] // c_here
    step = 8
    for i in range(0, bs, step):
        right = jnp.concatenate([ref[i + j] for j in range(step) for ref in piece_refs], axis=0)
        gram = lax.dot_general(
            left_ref[...], right, (((1,), (1,)), ((), ())), preferred_element_type=jnp.float32
        ).astype(jnp.bfloat16)
        for j in range(step):
            for c in range(c_here):
                out_ref[(i + j) * a_all : (i + j + 1) * a_all, c * d_all : (c + 1) * d_all] = gram[
                    c * a_all : (c + 1) * a_all, j * d_all : (j + 1) * d_all
                ]


def partial_integrals(left, pieces, c_all):
    rows, aux = left.shape
    a_all = rows // c_all
    bs, d_part, _ = pieces[0].shape
    d_all = d_part * len(pieces)
    piece_spec = pl.BlockSpec((bs, d_part, aux), lambda i: (0, 0, 0))
    return pl.pallas_call(
        integrals_kernel,
        grid=(c_all // CGROUP,),
        in_specs=[pl.BlockSpec((CGROUP * a_all, aux), lambda i: (i, 0))] + [piece_spec] * len(pieces),
        out_specs=pl.BlockSpec((bs * a_all, CGROUP * d_all), lambda i: (0, i)),
        out_shape=jax.ShapeDtypeStruct((bs * a_all, c_all * d_all), jnp.bfloat16),
        cost_estimate=pl.CostEstimate(
            flops=2 * rows * aux * bs * d_all,
            bytes_accessed=2 * (rows * aux + bs * d_all * (aux + rows)),
            transcendentals=0,
        ),
        compiler_params=pltpu.CompilerParams(vmem_limit_bytes=VMEM_BYTES),
        name="partial_integrals",
    )(left, *pieces)


def ladder_kernel(place_ref, integrals_ref, amps_ref, keep_ref, send_ref):
    high, quarter = keep_ref.shape[0], keep_ref.shape[-1]
    low = 2
    core, chip_x, near = place_ref[0], place_ref[1], place_ref[2]
    half = lax.dot_general(
        integrals_ref[...], amps_ref[...], (((1,), (1,)), ((), ())), preferred_element_type=jnp.float32
    ).astype(jnp.bfloat16)
    for h in range(high):
        slot = lax.rem(h - chip_x + high, high)
        blocks = [
            half[:, (h * low + c) * quarter : (h * low + c + 1) * quarter] for c in range(low)
        ]
        keep = jnp.where(core == 0, blocks[0], blocks[1])
        send = jnp.where(core == 0, blocks[1], blocks[0])
        if len(keep_ref.shape) == 3:
            keep_ref[slot], send_ref[slot] = keep, send
            continue
        _, inner, outer, bs, a_local, _ = keep_ref.shape
        a_all = outer * inner * a_local
        for i in range(inner):
            at = lax.rem(i - near + inner, inner)
            for b in range(bs):
                for o in range(outer):
                    row = b * a_all + (o * inner + i) * a_local
                    keep_ref[slot, at, o, b] = keep[row : row + a_local]
                    send_ref[slot, at, o, b] = send[row : row + a_local]


def ladder(place, integrals, amps, high, low, split):
    rows, inner = integrals.shape
    pairs = amps.shape[0]
    quarter = pairs // (high * low)
    block = ROW_BLOCK * 512 // max(512, pairs)
    if split[-1] % 16:
        shape, piece = (high, rows, quarter), (high, block, quarter)
        spec = pl.BlockSpec(piece, lambda i, place: (0, i, 0))
    else:
        near, far, a_local = split
        a_all = near * far * a_local
        shape = (high, near, far, rows // a_all, a_local, quarter)
        piece = (high, near, far, block // a_all, a_local, quarter)
        spec = pl.BlockSpec(piece, lambda i, place: (0, 0, 0, i, 0, 0))
    shape = jax.ShapeDtypeStruct(shape, jnp.bfloat16)
    return pl.pallas_call(
        ladder_kernel,
        grid_spec=pltpu.PrefetchScalarGridSpec(
            num_scalar_prefetch=1,
            grid=(rows // block,),
            in_specs=[
                pl.BlockSpec((block, inner), lambda i, place: (i, 0)),
                pl.BlockSpec((pairs, inner), lambda i, place: (0, 0), pipeline_mode=pl.Buffered(1)),
            ],
            out_specs=[spec, spec],
        ),
        out_shape=[shape, shape],
        cost_estimate=pl.CostEstimate(
            flops=2 * rows * inner * pairs,
            bytes_accessed=2 * (rows * inner + pairs * inner + rows * pairs),
            transcendentals=0,
        ),
        compiler_params=pltpu.CompilerParams(vmem_limit_bytes=VMEM_BYTES),
        name="ladder",
    )(place, integrals, amps)


def pick(x, index, axis):
    return lax.dynamic_index_in_dim(x, index, axis, keepdims=False)


def on_device(factors, amplitudes, tile_mask):
    aux, quarter, virtuals = factors.shape
    tiles, groups = lax.axis_size("tile"), lax.axis_size("grp")
    tile, grp = lax.axis_index("tile"), lax.axis_index("grp")
    low, inner = 2, 2
    high, outer = groups // low, tiles // inner
    core, chip_x = grp % low, grp // low
    near, far = tile % inner, tile // inner
    a_local = virtuals // tiles
    rows = amplitudes.shape[0]
    pairs = rows * tiles
    pair_quarter = pairs // groups
    f32, bf16 = jnp.float32, jnp.bfloat16
    if rows % IJB or VB % quarter or pair_quarter % IJB or VB % a_local or VB != NB:
        raise ValueError("block sizes")

    def shift(x, by_high=0, by_low=0, by_far=0, by_near=0):
        pairs_of = []
        for g in range(groups):
            for t in range(tiles):
                h, l = (g // low + by_high) % high, (g % low + by_low) % low
                o, i = (t // inner + by_far) % outer, (t % inner + by_near) % inner
                pairs_of.append((g * tiles + t, (h * low + l) * tiles + o * inner + i))
        return lax.ppermute(x, ("grp", "tile"), pairs_of)

    kept = lax.dynamic_slice_in_dim(tile_mask, tile * (rows // IJB), rows // IJB, 0)
    kept = pick(kept, grp * quarter // VB, 2).astype(bf16)[:, None, None, :, None]
    screened = amplitudes.reshape(rows // IJB, IJB, quarter, virtuals // VB, VB) * kept
    by_c = screened.reshape(rows, quarter, virtuals).transpose(2, 1, 0)
    by_c = by_c.reshape(high, low, quarter, quarter * rows)
    mine = pick(by_c, core, 1)
    theirs = shift(pick(by_c, 1 - core, 1), by_low=1)
    both = jnp.stack([mine, theirs])
    amp_pieces = []
    for k in range(high):
        part = pick(both, (chip_x + k) % high, 1)
        amp_pieces.append(shift(part, by_high=k) if k else part)

    window = factors[:, :, :NB].transpose(2, 1, 0)
    window, *amp_pieces = lax.optimization_barrier((window, *amp_pieces))

    amps = jnp.concatenate(amp_pieces).reshape(groups, quarter, quarter, rows)
    amps = amps.transpose(3, 1, 0, 2).reshape(rows, quarter * virtuals)
    amps = lax.all_gather(amps, "tile", axis=0, tiled=True)
    left = factors.reshape(aux, quarter * virtuals).T

    starts = [sum(SPLIT[:n]) for n in range(len(SPLIT))]
    owns = [window[s : s + size] for s, size in zip(starts, SPLIT)]
    others = []
    for n, own in enumerate(owns):
        others.append([])
        for k in range(1, high):
            others[n].append(shift(own, by_high=k))
    left, *others[0] = lax.optimization_barrier((left, *others[0]))
    integrals = []
    for n, own in enumerate(owns):
        held = [own] + others[n]
        if n:
            *held, integrals[-1] = lax.optimization_barrier((*held, integrals[-1]))
        pieces = []
        for piece in held:
            pieces += [piece, shift(piece, by_low=1)]
        integrals.append(partial_integrals(left, pieces, quarter))
    amps, *integrals = lax.optimization_barrier((amps, *integrals))

    place = jnp.stack([core, chip_x, near]).astype(jnp.int32)
    chunks = []
    for n, size in enumerate(SPLIT):
        keep, send = ladder(place, integrals[n], amps, high, low, (inner, outer, a_local))
        got = shift(send, by_low=1)
        parts = []
        for kx in range(high):
            for ky in range(inner):
                if keep.ndim == 6:
                    halves = [half[kx, ky] for half in (keep, got)]
                else:
                    view = (high, size, outer, inner, a_local, pair_quarter)
                    halves = [
                        pick(half.reshape(view)[kx], (near + ky) % inner, 2).swapaxes(0, 1)
                        for half in (keep, got)
                    ]
                parts.append((halves[0].astype(f32) + halves[1].astype(f32)).astype(bf16))
        if n + 1 < len(SPLIT):
            amps, *parts = lax.optimization_barrier((amps, *parts))
        total = None
        for kx in range(high):
            for ky in range(inner):
                part = parts[kx * inner + ky]
                if kx or ky:
                    part = shift(part, by_high=kx, by_near=ky)
                total = part.astype(f32) if total is None else total + part.astype(f32)
        total = total.astype(bf16)
        done = None
        for kz in range(outer):
            part = pick(total, (far + kz) % outer, 0)
            if kz:
                part = shift(part, by_far=kz)
            done = part.astype(f32) if done is None else done + part.astype(f32)
        chunks.append(done.transpose(1, 0, 2))
    summed = jnp.concatenate(chunks, axis=1)

    blocks = pair_quarter // IJB
    shown = lax.dynamic_slice_in_dim(tile_mask, grp * blocks, blocks, 0)[:, :, 0]
    shown = pick(shown, tile * a_local // VB, 1)
    shown = jnp.broadcast_to(shown[:, None], (blocks, IJB)).reshape(pair_quarter)
    return (summed * shown.astype(f32)).astype(bf16)


def solution(mesh):
    placed = (P("tile", "grp", None), P("tile", "grp", None), P())

    return jax.shard_map(
        on_device, mesh=mesh, in_specs=placed, out_specs=P("tile", None, "grp"), check_vma=False
    )
```

```python
import jax
import jax.numpy as jnp
from jax import lax
from jax.experimental import pallas as pl
from jax.experimental.pallas import tpu as pltpu
from jax.sharding import PartitionSpec as P


VB = 64
NB = 64
IJB = 64
SPLIT = (24, 24, 16)
CGROUP = 4
ROW_BLOCK = 512
VMEM_BYTES = 60 * 1024 * 1024


def integrals_kernel(*refs):
    left_ref, *piece_refs, out_ref = refs
    bs, d_part, _ = piece_refs[0].shape
    d_all = d_part * len(piece_refs)
    c_here = out_ref.shape[1] // d_all
    a_all = left_ref.shape[0] // c_here
    step = 8
    for i in range(0, bs, step):
        right = jnp.concatenate([ref[i + j] for j in range(step) for ref in piece_refs], axis=0)
        gram = lax.dot_general(
            left_ref[...], right, (((1,), (1,)), ((), ())), preferred_element_type=jnp.float32
        ).astype(jnp.bfloat16)
        for j in range(step):
            for c in range(c_here):
                out_ref[(i + j) * a_all : (i + j + 1) * a_all, c * d_all : (c + 1) * d_all] = gram[
                    c * a_all : (c + 1) * a_all, j * d_all : (j + 1) * d_all
                ]


def partial_integrals(left, pieces, c_all):
    rows, aux = left.shape
    a_all = rows // c_all
    bs, d_part, _ = pieces[0].shape
    d_all = d_part * len(pieces)
    piece_spec = pl.BlockSpec((bs, d_part, aux), lambda i: (0, 0, 0))
    return pl.pallas_call(
        integrals_kernel,
        grid=(c_all // CGROUP,),
        in_specs=[pl.BlockSpec((CGROUP * a_all, aux), lambda i: (i, 0))] + [piece_spec] * len(pieces),
        out_specs=pl.BlockSpec((bs * a_all, CGROUP * d_all), lambda i: (0, i)),
        out_shape=jax.ShapeDtypeStruct((bs * a_all, c_all * d_all), jnp.bfloat16),
        cost_estimate=pl.CostEstimate(
            flops=2 * rows * aux * bs * d_all,
            bytes_accessed=2 * (rows * aux + bs * d_all * (aux + rows)),
            transcendentals=0,
        ),
        compiler_params=pltpu.CompilerParams(vmem_limit_bytes=VMEM_BYTES),
        name="partial_integrals",
    )(left, *pieces)


def ladder_kernel(place_ref, mask_ref, integrals_ref, amps_ref, keep_ref, send_ref):
    high, _, quarter = keep_ref.shape
    low = 2
    core, chip_x = place_ref[0], place_ref[1]
    half = lax.dot_general(
        integrals_ref[...], amps_ref[...], (((1,), (1,)), ((), ())), preferred_element_type=jnp.float32
    ).astype(jnp.bfloat16)
    for h in range(high):
        slot = lax.rem(h - chip_x + high, high)
        blocks = [
            half[:, (h * low + c) * quarter : (h * low + c + 1) * quarter] for c in range(low)
        ]
        keep_ref[slot] = jnp.where(core == 0, blocks[0], blocks[1])
        send_ref[slot] = jnp.where(core == 0, blocks[1], blocks[0])


def tiled_ladder_kernel(
    place_ref, mask_ref, integrals_ref, amps_ref, keep_ref, send_ref, list_ref, full_ref
):
    high, inner, outer, bs, a_local, quarter = keep_ref.shape
    low = 2
    _, _, a_block, depth = integrals_ref.shape
    slots, few = list_ref.shape[0], list_ref.shape[0] // 2
    v_blocks = mask_ref.shape[0] // slots
    wide = round(v_blocks**0.5)
    core, chip_x, near, c_block = (place_ref[i] for i in range(4))
    a_at = pl.program_id(1)

    listed = jnp.int32(0)
    for n in range(slots):
        shown = mask_ref[n * v_blocks + a_at * wide] != 0
        kept = mask_ref[n * v_blocks + c_block * wide] != 0
        for d in range(1, wide):
            kept = jnp.logical_or(kept, mask_ref[n * v_blocks + c_block * wide + d] != 0)
        active = jnp.logical_and(shown, kept)
        list_ref[jnp.where(active, listed, slots - 1 - n + listed)] = jnp.int32(n)
        listed = listed + active.astype(jnp.int32)

    def product(amps):
        rows = integrals_ref[...].reshape(bs * a_block, depth)
        return lax.dot_general(
            rows, amps, (((1,), (1,)), ((), ())), preferred_element_type=jnp.float32
        ).astype(jnp.bfloat16)

    def emit(quarters):
        for h in range(high):
            slot = lax.rem(h - chip_x + high, high)
            first, second = quarters[h * low], quarters[h * low + 1]
            keep = jnp.where(core == 0, first, second)
            send = jnp.where(core == 0, second, first)
            for i in range(inner):
                at = lax.rem(i - near + inner, inner)
                for b in range(bs):
                    for o in range(outer):
                        row = b * a_block + (o * inner + i) * a_local
                        keep_ref[slot, at, o, b] = keep[row : row + a_local]
                        send_ref[slot, at, o, b] = send[row : row + a_local]

    @pl.when(listed <= few)
    def _():
        full_ref[...] = jnp.zeros_like(full_ref)
        at = [list_ref[n] for n in range(few)]
        some = product(
            jnp.concatenate(
                [amps_ref[pl.ds(pl.multiple_of(n * IJB, IJB), IJB), :] for n in at], axis=0
            )
        )
        per = quarter // IJB
        for n, index in enumerate(at):
            for k in range(per):

                @pl.when(lax.rem(index, per) == k)
                def _():
                    full_ref[lax.div(index, per), :, k * IJB : (k + 1) * IJB] = some[
                        :, n * IJB : (n + 1) * IJB
                    ]

        emit([full_ref[q] for q in range(high * low)])

    @pl.when(listed > few)
    def _():
        every = product(amps_ref[...])
        emit([every[:, q * quarter : (q + 1) * quarter] for q in range(high * low)])


def ladder(place, mask, integrals, amps, high, low, split):
    rows, inner = integrals.shape
    pairs = amps.shape[0]
    quarter = pairs // (high * low)
    near, far, a_local = split
    a_all = near * far * a_local
    amps_spec = pl.BlockSpec(
        (pairs, inner), lambda i, j, *_: (0, 0), pipeline_mode=pl.Buffered(1)
    )
    if a_local % 16 or quarter % 128 or VB % (near * a_local):
        block = ROW_BLOCK * 512 // max(512, pairs)
        kernel, grid, scratch = ladder_kernel, (rows // block, 1), []
        left_spec = pl.BlockSpec((block, inner), lambda i, j, *_: (i, 0))
        shape = (high, rows, quarter)
        spec = pl.BlockSpec((high, block, quarter), lambda i, j, *_: (0, i, 0))
    else:
        bs, parts = ROW_BLOCK // VB, a_all // VB
        kernel, grid = tiled_ladder_kernel, (rows // a_all // bs, parts)
        integrals = integrals.reshape(rows // a_all, parts, VB, inner)
        left_spec = pl.BlockSpec((bs, 1, VB, inner), lambda i, j, *_: (i, j, 0, 0))
        shape = (high, near, far, rows // a_all, a_local, quarter)
        piece = (high, near, far // parts, bs, a_local, quarter)
        spec = pl.BlockSpec(piece, lambda i, j, *_: (0, 0, j, i, 0, 0))
        scratch = [
            pltpu.SMEM((pairs // IJB,), jnp.int32),
            pltpu.VMEM((high * low, bs * VB, quarter), jnp.bfloat16),
        ]
    shape = jax.ShapeDtypeStruct(shape, jnp.bfloat16)
    return pl.pallas_call(
        kernel,
        grid_spec=pltpu.PrefetchScalarGridSpec(
            num_scalar_prefetch=2,
            grid=grid,
            in_specs=[left_spec, amps_spec],
            out_specs=[spec, spec],
            scratch_shapes=scratch,
        ),
        out_shape=[shape, shape],
        cost_estimate=pl.CostEstimate(
            flops=2 * rows * inner * pairs,
            bytes_accessed=2 * (rows * inner + pairs * inner + rows * pairs),
            transcendentals=0,
        ),
        compiler_params=pltpu.CompilerParams(vmem_limit_bytes=VMEM_BYTES),
        name="ladder",
    )(place, mask, integrals, amps)


def pick(x, index, axis):
    return lax.dynamic_index_in_dim(x, index, axis, keepdims=False)


def on_device(factors, amplitudes, tile_mask):
    aux, quarter, virtuals = factors.shape
    tiles, groups = lax.axis_size("tile"), lax.axis_size("grp")
    tile, grp = lax.axis_index("tile"), lax.axis_index("grp")
    low, inner = 2, 2
    high, outer = groups // low, tiles // inner
    core, chip_x = grp % low, grp // low
    near, far = tile % inner, tile // inner
    a_local = virtuals // tiles
    rows = amplitudes.shape[0]
    pairs = rows * tiles
    pair_quarter = pairs // groups
    f32, bf16 = jnp.float32, jnp.bfloat16
    if rows % IJB or VB % quarter or pair_quarter % IJB or VB % a_local or VB != NB:
        raise ValueError("block sizes")

    def shift(x, by_high=0, by_low=0, by_far=0, by_near=0):
        pairs_of = []
        for g in range(groups):
            for t in range(tiles):
                h, l = (g // low + by_high) % high, (g % low + by_low) % low
                o, i = (t // inner + by_far) % outer, (t % inner + by_near) % inner
                pairs_of.append((g * tiles + t, (h * low + l) * tiles + o * inner + i))
        return lax.ppermute(x, ("grp", "tile"), pairs_of)

    kept = lax.dynamic_slice_in_dim(tile_mask, tile * (rows // IJB), rows // IJB, 0)
    kept = pick(kept, grp * quarter // VB, 2).astype(bf16)[:, None, None, :, None]
    screened = amplitudes.reshape(rows // IJB, IJB, quarter, virtuals // VB, VB) * kept
    by_c = screened.reshape(rows, quarter, virtuals).transpose(2, 1, 0)
    by_c = by_c.reshape(high, low, quarter, quarter * rows)
    mine = pick(by_c, core, 1)
    theirs = shift(pick(by_c, 1 - core, 1), by_low=1)
    both = jnp.stack([mine, theirs])
    amp_pieces = []
    for k in range(high):
        part = pick(both, (chip_x + k) % high, 1)
        amp_pieces.append(shift(part, by_high=k) if k else part)

    window = factors[:, :, :NB].transpose(2, 1, 0)
    window, *amp_pieces = lax.optimization_barrier((window, *amp_pieces))

    amps = jnp.concatenate(amp_pieces).reshape(groups, quarter, quarter, rows)
    amps = amps.transpose(3, 1, 0, 2).reshape(rows, quarter * virtuals)
    amps = lax.all_gather(amps, "tile", axis=0, tiled=True)
    left = factors.reshape(aux, quarter * virtuals).T

    starts = [sum(SPLIT[:n]) for n in range(len(SPLIT))]
    owns = [window[s : s + size] for s, size in zip(starts, SPLIT)]
    others = []
    for n, own in enumerate(owns):
        others.append([])
        for k in range(1, high):
            others[n].append(shift(own, by_high=k))
    left, *others[0] = lax.optimization_barrier((left, *others[0]))
    integrals = []
    for n, own in enumerate(owns):
        held = [own] + others[n]
        if n:
            *held, integrals[-1] = lax.optimization_barrier((*held, integrals[-1]))
        pieces = []
        for piece in held:
            pieces += [piece, shift(piece, by_low=1)]
        integrals.append(partial_integrals(left, pieces, quarter))
    amps, *integrals = lax.optimization_barrier((amps, *integrals))

    place = jnp.stack([core, chip_x, near, grp * quarter // VB]).astype(jnp.int32)
    mask = tile_mask.reshape(-1)
    chunks = []
    for n, size in enumerate(SPLIT):
        keep, send = ladder(place, mask, integrals[n], amps, high, low, (inner, outer, a_local))
        got = shift(send, by_low=1)
        parts = []
        for kx in range(high):
            for ky in range(inner):
                if keep.ndim == 6:
                    halves = [half[kx, ky] for half in (keep, got)]
                else:
                    view = (high, size, outer, inner, a_local, pair_quarter)
                    halves = [
                        pick(half.reshape(view)[kx], (near + ky) % inner, 2).swapaxes(0, 1)
                        for half in (keep, got)
                    ]
                parts.append((halves[0].astype(f32) + halves[1].astype(f32)).astype(bf16))
        if n + 1 < len(SPLIT):
            amps, *parts = lax.optimization_barrier((amps, *parts))
        total = None
        for kx in range(high):
            for ky in range(inner):
                part = parts[kx * inner + ky]
                if kx or ky:
                    part = shift(part, by_high=kx, by_near=ky)
                total = part.astype(f32) if total is None else total + part.astype(f32)
        total = total.astype(bf16)
        done = None
        for kz in range(outer):
            part = pick(total, (far + kz) % outer, 0)
            if kz:
                part = shift(part, by_far=kz)
            done = part.astype(f32) if done is None else done + part.astype(f32)
        chunks.append(done.transpose(1, 0, 2))
    summed = jnp.concatenate(chunks, axis=1)

    blocks = pair_quarter // IJB
    shown = lax.dynamic_slice_in_dim(tile_mask, grp * blocks, blocks, 0)[:, :, 0]
    shown = pick(shown, tile * a_local // VB, 1)
    shown = jnp.broadcast_to(shown[:, None], (blocks, IJB)).reshape(pair_quarter)
    return (summed * shown.astype(f32)).astype(bf16)


def solution(mesh):
    placed = (P("tile", "grp", None), P("tile", "grp", None), P())

    return jax.shard_map(
        on_device, mesh=mesh, in_specs=placed, out_specs=P("tile", None, "grp"), check_vma=False
    )
```

```python
import jax
import jax.numpy as jnp
from jax import lax
from jax.experimental import pallas as pl
from jax.experimental.pallas import tpu as pltpu
from jax.sharding import PartitionSpec as P


VB = 64
NB = 64
IJB = 64
SPLIT = (24, 24, 16)
CGROUP = 4
ROW_BLOCK = 512
VMEM_BYTES = 60 * 1024 * 1024


def integrals_kernel(*refs):
    left_ref, *piece_refs, out_ref = refs
    bs, d_part, _ = piece_refs[0].shape
    d_all = d_part * len(piece_refs)
    c_here = out_ref.shape[1] // d_all
    a_all = left_ref.shape[0] // c_here
    step = 8
    for i in range(0, bs, step):
        right = jnp.concatenate([ref[i + j] for j in range(step) for ref in piece_refs], axis=0)
        gram = lax.dot_general(
            left_ref[...], right, (((1,), (1,)), ((), ())), preferred_element_type=jnp.float32
        ).astype(jnp.bfloat16)
        for j in range(step):
            for c in range(c_here):
                out_ref[(i + j) * a_all : (i + j + 1) * a_all, c * d_all : (c + 1) * d_all] = gram[
                    c * a_all : (c + 1) * a_all, j * d_all : (j + 1) * d_all
                ]


def partial_integrals(left, pieces, c_all):
    rows, aux = left.shape
    a_all = rows // c_all
    bs, d_part, _ = pieces[0].shape
    d_all = d_part * len(pieces)
    piece_spec = pl.BlockSpec((bs, d_part, aux), lambda i: (0, 0, 0))
    return pl.pallas_call(
        integrals_kernel,
        grid=(c_all // CGROUP,),
        in_specs=[pl.BlockSpec((CGROUP * a_all, aux), lambda i: (i, 0))] + [piece_spec] * len(pieces),
        out_specs=pl.BlockSpec((bs * a_all, CGROUP * d_all), lambda i: (0, i)),
        out_shape=jax.ShapeDtypeStruct((bs * a_all, c_all * d_all), jnp.bfloat16),
        cost_estimate=pl.CostEstimate(
            flops=2 * rows * aux * bs * d_all,
            bytes_accessed=2 * (rows * aux + bs * d_all * (aux + rows)),
            transcendentals=0,
        ),
        compiler_params=pltpu.CompilerParams(vmem_limit_bytes=VMEM_BYTES),
        name="partial_integrals",
    )(left, *pieces)


def ladder_kernel(place_ref, mask_ref, integrals_ref, amps_ref, keep_ref, send_ref):
    high, _, quarter = keep_ref.shape
    low = 2
    core, chip_x = place_ref[0], place_ref[1]
    half = lax.dot_general(
        integrals_ref[...], amps_ref[...], (((1,), (1,)), ((), ())), preferred_element_type=jnp.float32
    ).astype(jnp.bfloat16)
    for h in range(high):
        slot = lax.rem(h - chip_x + high, high)
        blocks = [
            half[:, (h * low + c) * quarter : (h * low + c + 1) * quarter] for c in range(low)
        ]
        keep_ref[slot] = jnp.where(core == 0, blocks[0], blocks[1])
        send_ref[slot] = jnp.where(core == 0, blocks[1], blocks[0])


def tiled_ladder_kernel(
    place_ref, mask_ref, integrals_ref, amps_ref, keep_ref, send_ref, list_ref, full_ref, some_ref
):
    high, inner, outer, bs, a_local, quarter = keep_ref.shape
    low = 2
    _, _, a_block, depth = integrals_ref.shape
    slots, few = list_ref.shape[0], list_ref.shape[0] // 2
    v_blocks = mask_ref.shape[0] // slots
    wide = round(v_blocks**0.5)
    core, chip_x, near, c_block = (place_ref[i] for i in range(4))
    a_at = pl.program_id(0)

    listed = jnp.int32(0)
    for n in range(slots):
        shown = mask_ref[n * v_blocks + a_at * wide] != 0
        kept = mask_ref[n * v_blocks + c_block * wide] != 0
        for d in range(1, wide):
            kept = jnp.logical_or(kept, mask_ref[n * v_blocks + c_block * wide + d] != 0)
        active = jnp.logical_and(shown, kept)
        list_ref[jnp.where(active, listed, slots - 1 - n + listed)] = jnp.int32(n)
        listed = listed + active.astype(jnp.int32)

    def product(amps):
        rows = integrals_ref[...].reshape(bs * a_block, depth)
        return lax.dot_general(
            rows, amps, (((1,), (1,)), ((), ())), preferred_element_type=jnp.float32
        ).astype(jnp.bfloat16)

    def emit(quarters):
        for h in range(high):
            slot = lax.rem(h - chip_x + high, high)
            first, second = quarters[h * low], quarters[h * low + 1]
            keep = jnp.where(core == 0, first, second)
            send = jnp.where(core == 0, second, first)
            for i in range(inner):
                at = lax.rem(i - near + inner, inner)
                for b in range(bs):
                    for o in range(outer):
                        row = b * a_block + (o * inner + i) * a_local
                        keep_ref[slot, at, o, b] = keep[row : row + a_local]
                        send_ref[slot, at, o, b] = send[row : row + a_local]

    @pl.when(listed <= few)
    def _():
        at = [list_ref[n] for n in range(few)]

        @pl.when(pl.program_id(1) == 0)
        def _():
            full_ref[...] = jnp.zeros_like(full_ref)
            for n, index in enumerate(at):
                start = pl.multiple_of(index * IJB, IJB)
                some_ref[n * IJB : (n + 1) * IJB, :] = amps_ref[pl.ds(start, IJB), :]

        some = product(some_ref[...])
        per = quarter // IJB
        for n, index in enumerate(at):
            for k in range(per):

                @pl.when(lax.rem(index, per) == k)
                def _():
                    full_ref[lax.div(index, per), :, k * IJB : (k + 1) * IJB] = some[
                        :, n * IJB : (n + 1) * IJB
                    ]

        emit([full_ref[q] for q in range(high * low)])

    @pl.when(listed > few)
    def _():
        every = product(amps_ref[...])
        emit([every[:, q * quarter : (q + 1) * quarter] for q in range(high * low)])


def ladder(place, mask, integrals, amps, high, low, split):
    rows, inner = integrals.shape
    pairs = amps.shape[0]
    quarter = pairs // (high * low)
    near, far, a_local = split
    a_all = near * far * a_local
    amps_spec = pl.BlockSpec(
        (pairs, inner), lambda i, j, *_: (0, 0), pipeline_mode=pl.Buffered(1)
    )
    if a_local % 16 or quarter % 128 or VB % (near * a_local):
        block = ROW_BLOCK * 512 // max(512, pairs)
        kernel, grid, scratch = ladder_kernel, (rows // block, 1), []
        left_spec = pl.BlockSpec((block, inner), lambda i, j, *_: (i, 0))
        shape = (high, rows, quarter)
        spec = pl.BlockSpec((high, block, quarter), lambda i, j, *_: (0, i, 0))
    else:
        bs, parts = ROW_BLOCK // VB, a_all // VB
        kernel, grid = tiled_ladder_kernel, (parts, rows // a_all // bs)
        integrals = integrals.reshape(rows // a_all, parts, VB, inner)
        left_spec = pl.BlockSpec((bs, 1, VB, inner), lambda j, i, *_: (i, j, 0, 0))
        shape = (high, near, far, rows // a_all, a_local, quarter)
        piece = (high, near, far // parts, bs, a_local, quarter)
        spec = pl.BlockSpec(piece, lambda j, i, *_: (0, 0, j, i, 0, 0))
        scratch = [
            pltpu.SMEM((pairs // IJB,), jnp.int32),
            pltpu.VMEM((high * low, bs * VB, quarter), jnp.bfloat16),
            pltpu.VMEM((pairs // 2, inner), jnp.bfloat16),
        ]
    shape = jax.ShapeDtypeStruct(shape, jnp.bfloat16)
    return pl.pallas_call(
        kernel,
        grid_spec=pltpu.PrefetchScalarGridSpec(
            num_scalar_prefetch=2,
            grid=grid,
            in_specs=[left_spec, amps_spec],
            out_specs=[spec, spec],
            scratch_shapes=scratch,
        ),
        out_shape=[shape, shape],
        cost_estimate=pl.CostEstimate(
            flops=2 * rows * inner * pairs,
            bytes_accessed=2 * (rows * inner + pairs * inner + rows * pairs),
            transcendentals=0,
        ),
        compiler_params=pltpu.CompilerParams(vmem_limit_bytes=VMEM_BYTES),
        name="ladder",
    )(place, mask, integrals, amps)


def pick(x, index, axis):
    return lax.dynamic_index_in_dim(x, index, axis, keepdims=False)


def on_device(factors, amplitudes, tile_mask):
    aux, quarter, virtuals = factors.shape
    tiles, groups = lax.axis_size("tile"), lax.axis_size("grp")
    tile, grp = lax.axis_index("tile"), lax.axis_index("grp")
    low, inner = 2, 2
    high, outer = groups // low, tiles // inner
    core, chip_x = grp % low, grp // low
    near, far = tile % inner, tile // inner
    a_local = virtuals // tiles
    rows = amplitudes.shape[0]
    pairs = rows * tiles
    pair_quarter = pairs // groups
    f32, bf16 = jnp.float32, jnp.bfloat16
    if rows % IJB or VB % quarter or pair_quarter % IJB or VB % a_local or VB != NB:
        raise ValueError("block sizes")

    def shift(x, by_high=0, by_low=0, by_far=0, by_near=0):
        pairs_of = []
        for g in range(groups):
            for t in range(tiles):
                h, l = (g // low + by_high) % high, (g % low + by_low) % low
                o, i = (t // inner + by_far) % outer, (t % inner + by_near) % inner
                pairs_of.append((g * tiles + t, (h * low + l) * tiles + o * inner + i))
        return lax.ppermute(x, ("grp", "tile"), pairs_of)

    kept = lax.dynamic_slice_in_dim(tile_mask, tile * (rows // IJB), rows // IJB, 0)
    kept = pick(kept, grp * quarter // VB, 2).astype(bf16)[:, None, None, :, None]
    screened = amplitudes.reshape(rows // IJB, IJB, quarter, virtuals // VB, VB) * kept
    by_c = screened.reshape(rows, quarter, virtuals).transpose(2, 1, 0)
    by_c = by_c.reshape(high, low, quarter, quarter * rows)
    mine = pick(by_c, core, 1)
    theirs = shift(pick(by_c, 1 - core, 1), by_low=1)
    both = jnp.stack([mine, theirs])
    amp_pieces = []
    for k in range(high):
        part = pick(both, (chip_x + k) % high, 1)
        amp_pieces.append(shift(part, by_high=k) if k else part)

    window = factors[:, :, :NB].transpose(2, 1, 0)
    window, *amp_pieces = lax.optimization_barrier((window, *amp_pieces))

    amps = jnp.concatenate(amp_pieces).reshape(groups, quarter, quarter, rows)
    amps = amps.transpose(3, 1, 0, 2).reshape(rows, quarter * virtuals)
    amps = lax.all_gather(amps, "tile", axis=0, tiled=True)
    left = factors.reshape(aux, quarter * virtuals).T

    starts = [sum(SPLIT[:n]) for n in range(len(SPLIT))]
    owns = [window[s : s + size] for s, size in zip(starts, SPLIT)]
    others = []
    for n, own in enumerate(owns):
        others.append([])
        for k in range(1, high):
            others[n].append(shift(own, by_high=k))
    left, *others[0] = lax.optimization_barrier((left, *others[0]))
    integrals = []
    for n, own in enumerate(owns):
        held = [own] + others[n]
        if n:
            *held, integrals[-1] = lax.optimization_barrier((*held, integrals[-1]))
        pieces = []
        for piece in held:
            pieces += [piece, shift(piece, by_low=1)]
        integrals.append(partial_integrals(left, pieces, quarter))
    amps, *integrals = lax.optimization_barrier((amps, *integrals))

    place = jnp.stack([core, chip_x, near, grp * quarter // VB]).astype(jnp.int32)
    mask = tile_mask.reshape(-1)
    chunks = []
    for n, size in enumerate(SPLIT):
        keep, send = ladder(place, mask, integrals[n], amps, high, low, (inner, outer, a_local))
        got = shift(send, by_low=1)
        parts = []
        for kx in range(high):
            for ky in range(inner):
                if keep.ndim == 6:
                    halves = [half[kx, ky] for half in (keep, got)]
                else:
                    view = (high, size, outer, inner, a_local, pair_quarter)
                    halves = [
                        pick(half.reshape(view)[kx], (near + ky) % inner, 2).swapaxes(0, 1)
                        for half in (keep, got)
                    ]
                parts.append((halves[0].astype(f32) + halves[1].astype(f32)).astype(bf16))
        if n + 1 < len(SPLIT):
            amps, *parts = lax.optimization_barrier((amps, *parts))
        total = None
        for kx in range(high):
            for ky in range(inner):
                part = parts[kx * inner + ky]
                if kx or ky:
                    part = shift(part, by_high=kx, by_near=ky)
                total = part.astype(f32) if total is None else total + part.astype(f32)
        total = total.astype(bf16)
        done = None
        for kz in range(outer):
            part = pick(total, (far + kz) % outer, 0)
            if kz:
                part = shift(part, by_far=kz)
            done = part.astype(f32) if done is None else done + part.astype(f32)
        chunks.append(done.transpose(1, 0, 2))
    summed = jnp.concatenate(chunks, axis=1)

    blocks = pair_quarter // IJB
    shown = lax.dynamic_slice_in_dim(tile_mask, grp * blocks, blocks, 0)[:, :, 0]
    shown = pick(shown, tile * a_local // VB, 1)
    shown = jnp.broadcast_to(shown[:, None], (blocks, IJB)).reshape(pair_quarter)
    return (summed * shown.astype(f32)).astype(bf16)


def solution(mesh):
    placed = (P("tile", "grp", None), P("tile", "grp", None), P())

    return jax.shard_map(
        on_device, mesh=mesh, in_specs=placed, out_specs=P("tile", None, "grp"), check_vma=False
    )
```
